32 devices in a mesh: row: 4 (over x, core), col: 2 (over y), fiber: 4 (over z).
Axes of the slice: x: 2, y: 2, z: 4, core: 2. Of those that a mesh axis runs over, the one named last changes fastest.
Arguments:
- values: float32 [3072, 3072], P('row', ('col', 'fiber')), may hold values from -6 to 6
- tile_mask: int32 [24, 24], P('row', ('col', 'fiber')), may hold values from 0 to 1, as said below
- keep_mask: int32 [24, 24], P('row', ('col', 'fiber')), may hold values 0 or 1
Outputs:
- flows: float32 [3072, 3072], P('row', ('col', 'fiber'))
The draws below stay inside these ranges and needn't reach their ends.
Inputs may be any that keep to these rules, and one draw needn't show every extreme that they name: `tile_mask`: 1 marks a tile that holds entries; every diagonal tile is 1, and tiles with low indices are denser.
All inputs are finite; a program needn't handle non-finite values. No bound on the sum of `keep_mask` on one device may be relied on, other than what follows from the above.
Results may differ from the reference program's by a relative error of at most 0.017.
Values may be sent and summed in bfloat16 or wider, within the bound.
A program may use at most 64 MiB of HBM per device.

```python
import jax
import jax.numpy as jnp
from jax import lax

UNIT = 384
N = 3072
NTILES = 24
N_FIBER = 4


def draw_tile_mask(key, part):
    indices = jnp.arange(NTILES, dtype=jnp.int32)
    row_ids = indices[:, None]
    col_ids = indices[None, :]
    levels = max(1, (NTILES - 1).bit_length())
    agreement = jnp.zeros((NTILES, NTILES), jnp.int32)
    both_low = jnp.zeros((NTILES, NTILES), jnp.int32)
    for level in range(levels):
        row_bit = row_ids >> level & 1
        col_bit = col_ids >> level & 1
        agreement = agreement + (row_bit == col_bit).astype(jnp.int32)
        both_low = both_low + ((row_bit == 0) & (col_bit == 0)).astype(jnp.int32)
    ticket = jax.random.randint(jax.random.fold_in(key, 17), (NTILES, NTILES), 0, 2 * levels + 1)
    kept_tiles = (ticket <= agreement + both_low) | (row_ids == col_ids)
    return kept_tiles.astype(jnp.int32)


def place_ends(values, stream_key, smallest, largest):
    longest = values.shape.index(max(values.shape))
    spots = []
    for shift in (0, 1):
        where = [jax.random.randint(jax.random.fold_in(stream_key, axis), (), 0, length) for axis, length in enumerate(values.shape)]
        where[longest] = (where[longest] + shift) % values.shape[longest]
        spots.append(tuple(where))
    return values.at[spots[0]].set(smallest).at[spots[1]].set(largest)


def steps_of(stream_key, extent, cuts, low, top_value):
    gain, own = 1.0, jax.random.fold_in(stream_key, 6)
    for axis_at, parts in cuts:
        draws = jnp.exp(jax.random.uniform(jax.random.fold_in(own, axis_at), (parts,), jnp.float32, low / len(cuts), top_value / len(cuts)))
        gain = gain * jnp.repeat(draws, extent[axis_at] // parts).reshape([-1 if axis == axis_at else 1 for axis in range(len(extent))])
    return gain


def scatter_about(rng, dims, spread, most, split=(), held_as=jnp.bfloat16):
    level = steps_of(rng, dims, split, -0.22, 0.18) if split else 1.0
    result = jax.random.normal(rng, dims, jnp.float32) * spread * level
    return jnp.minimum(jnp.maximum(result, -most), most).astype(held_as)


def setup_inputs(seed: int = 0) -> dict:
    seeds = jax.random.split(jax.random.key(seed), 4)
    return {
        "values": scatter_about(seeds[0], (N, N), 1.0, 6.0, ((0, 4), (1, 8)), jnp.float32),
        "tile_mask": draw_tile_mask(jax.random.fold_in(seeds[3], 71), 0),
        "keep_mask": place_ends((jax.random.randint(seeds[2], (NTILES, NTILES), 0, 4) < 3).astype(jnp.int32), jax.random.fold_in(seeds[2], 1), 0, 1),
    }


def spread_tiles(mask, tile_size):
    count_rows, count_cols = mask.shape
    wide = jnp.broadcast_to(mask.astype(jnp.float32)[:, None, :, None], (count_rows, tile_size, count_cols, tile_size))
    return wide.reshape(count_rows * tile_size, count_cols * tile_size)


def reference(values, tile_mask, keep_mask):
    tile_size = values.shape[0] // tile_mask.shape[0]
    total = values.shape[0]
    sub_width = UNIT // N_FIBER
    weighted = (values * spread_tiles(tile_mask, tile_size)).astype(jnp.bfloat16)
    layer_cols = weighted.reshape(total, total // UNIT, N_FIBER, sub_width)
    layer_rows = weighted.reshape(total // UNIT, N_FIBER, sub_width, total)

    def add_layer(layer, running):
        left_part = lax.dynamic_index_in_dim(layer_cols, layer, 2, keepdims=False).reshape(total, (total // UNIT) * sub_width)
        right_part = lax.dynamic_index_in_dim(layer_rows, layer, 1, keepdims=False).reshape((total // UNIT) * sub_width, total)
        product = jnp.dot(left_part, right_part, preferred_element_type=jnp.float32)
        return running + product.astype(jnp.bfloat16).astype(jnp.float32)

    expanded = lax.fori_loop(0, N_FIBER, add_layer, jnp.zeros((total, total), jnp.float32))
    squared = expanded * expanded
    col_scale = jnp.mean(squared, axis=0) + 1e-6
    return spread_tiles(keep_mask, tile_size) * squared / col_scale[None, :]
```

```python
import functools

import jax
import jax.numpy as jnp
from jax import lax
from jax.experimental import pallas as pl
from jax.experimental.pallas import tpu as pltpu
from jax.sharding import PartitionSpec as P

MESH = pl.DeviceIdType.MESH
CHUNKS = 4


def kernel(
    n_row, n_col, n_fib, tile_ref, keep_ref, values_ref, out_ref,
    left, right, own, part_out, part_in, sums,
    send_up, send_down, recv_left, send_right, recv_right, send_pair, recv_pair,
    send_part, recv_part, send_sum, recv_sum,
):
    r, c, f = lax.axis_index("row"), lax.axis_index("col"), lax.axis_index("fiber")
    rows, unit = values_ref.shape
    tile = unit // tile_ref.shape[1]
    step = rows // CHUNKS
    group = n_row // n_col
    owner, seat = r // group, lax.rem(r, group)

    barrier = pltpu.get_barrier_semaphore()
    for dr in range(n_row):
        for dc in range(n_col):
            if dr or dc:
                pl.semaphore_signal(
                    barrier, inc=1, device_id_type=MESH,
                    device_id=(lax.rem(r + dr, n_row), lax.rem(c + dc, n_col), f),
                )

    has_down, has_up = f > 0, f < n_fib - 1

    @pl.when(has_down)
    def _():
        pl.semaphore_signal(barrier, inc=1, device_id=(r, c, f - 1), device_id_type=MESH)

    @pl.when(has_up)
    def _():
        pl.semaphore_signal(barrier, inc=1, device_id=(r, c, f + 1), device_id_type=MESH)

    for i in range(rows // tile):
        for j in range(unit // tile):
            at = (pl.ds(i * tile, tile), pl.ds(j * tile, tile))
            masked = values_ref[at] * tile_ref[i, j].astype(jnp.float32)
            left[f, i * tile:(i + 1) * tile, j * tile:(j + 1) * tile] = masked.astype(jnp.bfloat16)

    neighbours = has_down.astype(jnp.int32) + has_up.astype(jnp.int32)
    pl.semaphore_wait(barrier, n_row * n_col - 1 + neighbours)

    def along(source, i, up):
        part = left.at[source, pl.ds(pl.multiple_of(i * step, step), step)]
        return pltpu.make_async_remote_copy(
            src_ref=part, dst_ref=part,
            send_sem=(send_up if up else send_down).at[source, i],
            recv_sem=recv_left.at[source, i],
            device_id=(r, c, f + 1 if up else f - 1), device_id_type=MESH,
        )

    def right_at(col, place):
        return right.at[
            pl.ds(pl.multiple_of(place * rows, rows), rows),
            pl.ds(pl.multiple_of(col * unit, unit), unit),
        ]

    def to_right(t):
        return pltpu.make_async_remote_copy(
            src_ref=left.at[f], dst_ref=right_at(c, seat),
            send_sem=send_right.at[t], recv_sem=recv_right.at[c],
            device_id=(t * group + seat, owner, f), device_id_type=MESH,
        )

    def came_right(col):
        return pltpu.make_async_remote_copy(
            src_ref=left.at[f], dst_ref=right_at(col, seat),
            send_sem=send_right.at[0], recv_sem=recv_right.at[col],
            device_id=(r, c, f), device_id_type=MESH,
        )

    def to_pair(col, other):
        return pltpu.make_async_remote_copy(
            src_ref=right_at(col, seat), dst_ref=right_at(col, seat),
            send_sem=send_pair.at[col, other], recv_sem=recv_pair.at[col, seat],
            device_id=(owner * group + other, c, f), device_id_type=MESH,
        )

    def came_pair(col, other):
        return pltpu.make_async_remote_copy(
            src_ref=right_at(col, other), dst_ref=right_at(col, other),
            send_sem=send_pair.at[col, other], recv_sem=recv_pair.at[col, other],
            device_id=(r, c, f), device_id_type=MESH,
        )

    def to_col(col, i):
        part = pl.ds(pl.multiple_of(i * step, step), step)
        return pltpu.make_async_remote_copy(
            src_ref=part_out.at[col, part], dst_ref=part_in.at[c, part],
            send_sem=send_part.at[col, i], recv_sem=recv_part.at[c, i],
            device_id=(r, col, f), device_id_type=MESH,
        )

    def came_col(col, i):
        part = pl.ds(pl.multiple_of(i * step, step), step)
        return pltpu.make_async_remote_copy(
            src_ref=part_out.at[col, part], dst_ref=part_in.at[col, part],
            send_sem=send_part.at[col, i], recv_sem=recv_part.at[col, i],
            device_id=(r, col, f), device_id_type=MESH,
        )

    @pl.loop(0, CHUNKS)
    def _(i):
        @pl.when(has_down)
        def _():
            along(f, i, False).start()

        @pl.when(has_up)
        def _():
            along(f, i, True).start()

    mine = owner == c
    for t in range(n_row // group):
        @pl.when(jnp.logical_not(mine & (owner == t)))
        def _():
            to_right(t).start()

    @pl.when(mine)
    def _():
        spot = right_at(c, seat)
        spot[...] = left[f]

    def relay(d, i):
        @pl.when(f - d >= 0)
        def _():
            along(f - d, i, True).wait_recv()

            @pl.when(has_up)
            def _():
                along(f - d, i, True).start()

        @pl.when(f + d < n_fib)
        def _():
            along(f + d, i, False).wait_recv()

            @pl.when(has_down)
            def _():
                along(f + d, i, False).start()

    def gather_right():
        for col in range(n_col):
            @pl.when(jnp.logical_not(mine & (c == col)))
            def _():
                came_right(col).wait_recv()

            for other in range(group):
                @pl.when(seat != other)
                def _():
                    to_pair(col, other).start()

    for d in range(1, n_fib - 1):
        @pl.loop(0, CHUNKS)
        def _(i):
            relay(d, i)

        if d == 1:
            gather_right()
    if n_fib < 3:
        gather_right()

    for col in range(n_col):
        for other in range(group):
            @pl.when(seat != other)
            def _():
                came_pair(col, other).wait_recv()

    @pl.loop(0, CHUNKS)
    def _(i):
        if n_fib > 1:
            relay(n_fib - 1, i)
        part = pl.ds(pl.multiple_of(i * step, step), step)
        for col in range(n_col):
            product = jnp.zeros((step, unit), jnp.float32)
            for k in range(n_fib):
                product += jnp.dot(
                    left[k, part, :],
                    right[k * unit:(k + 1) * unit, col * unit:(col + 1) * unit],
                    preferred_element_type=jnp.float32,
                )

            @pl.when(c == col)
            def _():
                own[part, :] = product

            @pl.when(c != col)
            def _():
                part_out[col, part, :] = product.astype(jnp.bfloat16)
                to_col(col, i).start()

    column = jnp.zeros((8, unit), jnp.float32)
    for i in range(CHUNKS):
        at = slice(i * step, (i + 1) * step)
        for shift in range(1, n_col):
            col = lax.rem(c + shift, n_col)
            came_col(col, i).wait_recv()
            own[at, :] += part_in[col, at, :].astype(jnp.float32)
        squared = own[at, :] * own[at, :]
        own[at, :] = squared
        column += jnp.sum(squared.reshape(step // 8, 8, unit), axis=0)
    sums[r] = column

    def to_row(shift):
        return pltpu.make_async_remote_copy(
            src_ref=sums.at[r], dst_ref=sums.at[r],
            send_sem=send_sum.at[shift], recv_sem=recv_sum.at[r],
            device_id=(lax.rem(r + shift, n_row), c, f), device_id_type=MESH,
        )

    def came_row(other):
        return pltpu.make_async_remote_copy(
            src_ref=sums.at[r], dst_ref=sums.at[other],
            send_sem=send_sum.at[0], recv_sem=recv_sum.at[other],
            device_id=(other, c, f), device_id_type=MESH,
        )

    for shift in range(1, n_row):
        to_row(shift).start()
    for shift in range(1, n_row):
        came_row(lax.rem(r + shift, n_row)).wait_recv()
    total = sums[0]
    for other in range(1, n_row):
        total += sums[other]
    scale = jnp.sum(total, axis=0, keepdims=True) / (rows * n_row) + 1e-6
    inverse = 1.0 / scale
    for i in range(rows // tile):
        for j in range(unit // tile):
            at = (slice(i * tile, (i + 1) * tile), slice(j * tile, (j + 1) * tile))
            out_ref[at] = own[at] * (inverse[:, at[1]] * keep_ref[i, j].astype(jnp.float32))

    @pl.loop(0, CHUNKS)
    def _(i):
        for source in range(n_fib):
            @pl.when(has_up & (source <= f))
            def _():
                along(source, i, True).wait_send()

            @pl.when(has_down & (source >= f))
            def _():
                along(source, i, False).wait_send()

        for shift in range(1, n_col):
            to_col(lax.rem(c + shift, n_col), i).wait_send()

    for t in range(n_row // group):
        @pl.when(jnp.logical_not(mine & (owner == t)))
        def _():
            to_right(t).wait_send()

    for col in range(n_col):
        for other in range(group):
            @pl.when(seat != other)
            def _():
                to_pair(col, other).wait_send()

    for shift in range(1, n_row):
        to_row(shift).wait_send()


def solution(mesh):
    n_row, n_col, n_fib = (mesh.shape[name] for name in ("row", "col", "fiber"))
    group = n_row // n_col

    def local(values, tile_mask, keep_mask):
        rows, unit = values.shape
        dma = pltpu.SemaphoreType.DMA
        return pl.pallas_call(
            functools.partial(kernel, n_row, n_col, n_fib),
            out_shape=jax.ShapeDtypeStruct((rows, unit), jnp.float32),
            in_specs=[
                pl.BlockSpec(memory_space=pltpu.SMEM),
                pl.BlockSpec(memory_space=pltpu.SMEM),
                pl.BlockSpec(memory_space=pltpu.VMEM),
            ],
            out_specs=pl.BlockSpec(memory_space=pltpu.VMEM),
            scratch_shapes=[
                pltpu.VMEM((n_fib, rows, unit), jnp.bfloat16),
                pltpu.VMEM((group * rows, n_col * unit), jnp.bfloat16),
                pltpu.VMEM((rows, unit), jnp.float32),
                pltpu.VMEM((n_col, rows, unit), jnp.bfloat16),
                pltpu.VMEM((n_col, rows, unit), jnp.bfloat16),
                pltpu.VMEM((n_row, 8, unit), jnp.float32),
                dma((n_fib, CHUNKS)),
                dma((n_fib, CHUNKS)),
                dma((n_fib, CHUNKS)),
                dma((n_row // group,)),
                dma((n_col,)),
                dma((n_col, group)),
                dma((n_col, group)),
                dma((n_col, CHUNKS)),
                dma((n_col, CHUNKS)),
                dma((n_row,)),
                dma((n_row,)),
            ],
            compiler_params=pltpu.CompilerParams(collective_id=0, has_side_effects=True),
        )(tile_mask, keep_mask, values)

    spec = P("row", ("col", "fiber"))
    return jax.shard_map(
        local, mesh=mesh, in_specs=(spec, spec, spec), out_specs=spec, check_vma=False
    )
```

```python
import functools

import jax
import jax.numpy as jnp
from jax import lax
from jax.experimental import pallas as pl
from jax.experimental.pallas import tpu as pltpu
from jax.sharding import PartitionSpec as P

MESH = pl.DeviceIdType.MESH
CHUNKS = 6
VMEM_LIMIT = 62 * 1024 * 1024


def kernel(
    n_row, n_col, n_fib, tile_hbm, values_hbm, own, inverse_ref,
    tile_ref, values_ref, left, right, part_out, part_in, sums, load_sem,
    send_up, send_down, recv_left, send_right, recv_right, send_pair, recv_pair,
    send_part, recv_part, send_sum, recv_sum,
):
    r, c, f = lax.axis_index("row"), lax.axis_index("col"), lax.axis_index("fiber")
    rows, unit = values_ref.shape
    tile = unit // tile_ref.shape[0]
    step = rows // CHUNKS
    group = n_row // n_col
    owner, seat = r // group, lax.rem(r, group)

    load = pltpu.make_async_copy(values_hbm, values_ref, load_sem.at[0])
    load.start()
    load_tile = pltpu.make_async_copy(tile_hbm, tile_ref, load_sem.at[1])
    load_tile.start()

    barrier = pltpu.get_barrier_semaphore()
    for dr in range(n_row):
        for dc in range(n_col):
            if dr or dc:
                pl.semaphore_signal(
                    barrier, inc=1, device_id_type=MESH,
                    device_id=(lax.rem(r + dr, n_row), lax.rem(c + dc, n_col), f),
                )

    has_down, has_up = f > 0, f < n_fib - 1

    @pl.when(has_down)
    def _():
        pl.semaphore_signal(barrier, inc=1, device_id=(r, c, f - 1), device_id_type=MESH)

    @pl.when(has_up)
    def _():
        pl.semaphore_signal(barrier, inc=1, device_id=(r, c, f + 1), device_id_type=MESH)

    load_tile.wait()
    load.wait()

    for i in range(rows // tile):
        for j in range(unit // tile):
            at = (pl.ds(i * tile, tile), pl.ds(j * tile, tile))
            masked = values_ref[at] * tile_ref[j, i].astype(jnp.float32)
            left[f, i * tile:(i + 1) * tile, j * tile:(j + 1) * tile] = masked.astype(jnp.bfloat16)

    neighbours = has_down.astype(jnp.int32) + has_up.astype(jnp.int32)
    pl.semaphore_wait(barrier, n_row * n_col - 1 + neighbours)

    def along(source, i, up):
        part = left.at[source, pl.ds(pl.multiple_of(i * step, step), step)]
        return pltpu.make_async_remote_copy(
            src_ref=part, dst_ref=part,
            send_sem=(send_up if up else send_down).at[source, i],
            recv_sem=recv_left.at[source, i],
            device_id=(r, c, f + 1 if up else f - 1), device_id_type=MESH,
        )

    def right_at(col, place):
        return right.at[
            pl.ds(pl.multiple_of(place * rows, rows), rows),
            pl.ds(pl.multiple_of(col * unit, unit), unit),
        ]

    def to_right(t):
        return pltpu.make_async_remote_copy(
            src_ref=left.at[f], dst_ref=right_at(c, seat),
            send_sem=send_right.at[t], recv_sem=recv_right.at[c],
            device_id=(t * group + seat, owner, f), device_id_type=MESH,
        )

    def came_right(col):
        return pltpu.make_async_remote_copy(
            src_ref=left.at[f], dst_ref=right_at(col, seat),
            send_sem=send_right.at[0], recv_sem=recv_right.at[col],
            device_id=(r, c, f), device_id_type=MESH,
        )

    def to_pair(col, other):
        return pltpu.make_async_remote_copy(
            src_ref=right_at(col, seat), dst_ref=right_at(col, seat),
            send_sem=send_pair.at[col, other], recv_sem=recv_pair.at[col, seat],
            device_id=(owner * group + other, c, f), device_id_type=MESH,
        )

    def came_pair(col, other):
        return pltpu.make_async_remote_copy(
            src_ref=right_at(col, other), dst_ref=right_at(col, other),
            send_sem=send_pair.at[col, other], recv_sem=recv_pair.at[col, other],
            device_id=(r, c, f), device_id_type=MESH,
        )

    def to_col(col, i):
        part = pl.ds(pl.multiple_of(i * step, step), step)
        return pltpu.make_async_remote_copy(
            src_ref=part_out.at[col, part], dst_ref=part_in.at[c, part],
            send_sem=send_part.at[col, i], recv_sem=recv_part.at[c, i],
            device_id=(r, col, f), device_id_type=MESH,
        )

    def came_col(col, i):
        part = pl.ds(pl.multiple_of(i * step, step), step)
        return pltpu.make_async_remote_copy(
            src_ref=part_out.at[col, part], dst_ref=part_in.at[col, part],
            send_sem=send_part.at[col, i], recv_sem=recv_part.at[col, i],
            device_id=(r, col, f), device_id_type=MESH,
        )

    @pl.loop(0, CHUNKS)
    def _(i):
        @pl.when(has_down)
        def _():
            along(f, i, False).start()

        @pl.when(has_up)
        def _():
            along(f, i, True).start()

    mine = owner == c
    for t in range(n_row // group):
        @pl.when(jnp.logical_not(mine & (owner == t)))
        def _():
            to_right(t).start()

    @pl.when(mine)
    def _():
        spot = right_at(c, seat)
        spot[...] = left[f]

    def relay(d, i):
        @pl.when(f - d >= 0)
        def _():
            along(f - d, i, True).wait_recv()

            @pl.when(has_up)
            def _():
                along(f - d, i, True).start()

        @pl.when(f + d < n_fib)
        def _():
            along(f + d, i, False).wait_recv()

            @pl.when(has_down)
            def _():
                along(f + d, i, False).start()

    def gather_right():
        for col in range(n_col):
            @pl.when(jnp.logical_not(mine & (c == col)))
            def _():
                came_right(col).wait_recv()

            for other in range(group):
                @pl.when(seat != other)
                def _():
                    to_pair(col, other).start()

    for d in range(1, n_fib - 1):
        @pl.loop(0, CHUNKS)
        def _(i):
            relay(d, i)

        if d == 1:
            gather_right()
    if n_fib < 3:
        gather_right()

    for col in range(n_col):
        for other in range(group):
            @pl.when(seat != other)
            def _():
                came_pair(col, other).wait_recv()

    @pl.loop(0, CHUNKS)
    def _(i):
        if n_fib > 1:
            relay(n_fib - 1, i)
        part = pl.ds(pl.multiple_of(i * step, step), step)
        for col in range(n_col):
            product = jnp.zeros((step, unit), jnp.float32)
            for k in range(n_fib):
                product += jnp.dot(
                    left[k, part, :],
                    right[k * unit:(k + 1) * unit, col * unit:(col + 1) * unit],
                    preferred_element_type=jnp.float32,
                )

            @pl.when(c == col)
            def _():
                own[part, :] = product

            @pl.when(c != col)
            def _():
                part_out[col, part, :] = product.astype(jnp.bfloat16)
                to_col(col, i).start()

    column = jnp.zeros((8, unit), jnp.float32)
    for i in range(CHUNKS):
        at = slice(i * step, (i + 1) * step)
        for shift in range(1, n_col):
            col = lax.rem(c + shift, n_col)
            came_col(col, i).wait_recv()
            own[at, :] += part_in[col, at, :].astype(jnp.float32)
        squared = own[at, :] * own[at, :]
        own[at, :] = squared
        column += jnp.sum(squared.reshape(step // 8, 8, unit), axis=0)
    sums[r] = column

    def to_row(shift):
        return pltpu.make_async_remote_copy(
            src_ref=sums.at[r], dst_ref=sums.at[r],
            send_sem=send_sum.at[shift], recv_sem=recv_sum.at[r],
            device_id=(lax.rem(r + shift, n_row), c, f), device_id_type=MESH,
        )

    def came_row(other):
        return pltpu.make_async_remote_copy(
            src_ref=sums.at[r], dst_ref=sums.at[other],
            send_sem=send_sum.at[0], recv_sem=recv_sum.at[other],
            device_id=(other, c, f), device_id_type=MESH,
        )

    for shift in range(1, n_row):
        to_row(shift).start()
    for shift in range(1, n_row):
        came_row(lax.rem(r + shift, n_row)).wait_recv()
    total = sums[0]
    for other in range(1, n_row):
        total += sums[other]
    scale = jnp.sum(total, axis=0, keepdims=True) / (rows * n_row) + 1e-6
    inverse_ref[...] = jnp.broadcast_to(1.0 / scale, inverse_ref.shape)

    @pl.loop(0, CHUNKS)
    def _(i):
        for source in range(n_fib):
            @pl.when(has_up & (source <= f))
            def _():
                along(source, i, True).wait_send()

            @pl.when(has_down & (source >= f))
            def _():
                along(source, i, False).wait_send()

        for shift in range(1, n_col):
            to_col(lax.rem(c + shift, n_col), i).wait_send()

    for t in range(n_row // group):
        @pl.when(jnp.logical_not(mine & (owner == t)))
        def _():
            to_right(t).wait_send()

    for col in range(n_col):
        for other in range(group):
            @pl.when(seat != other)
            def _():
                to_pair(col, other).wait_send()

    for shift in range(1, n_row):
        to_row(shift).wait_send()


def prune(keep_ref, squared_ref, inverse_ref, out_hbm, out_vmem, sem):
    tile = out_vmem.shape[1] // keep_ref.shape[0]
    copies = []
    for i in range(keep_ref.shape[1]):
        down = slice(i * tile, (i + 1) * tile)
        for j in range(keep_ref.shape[0]):
            across = slice(j * tile, (j + 1) * tile)
            factor = inverse_ref[0:1, across] * keep_ref[j, i].astype(jnp.float32)
            out_vmem[down, across] = squared_ref[down, across] * factor
        copy = pltpu.make_async_copy(out_vmem.at[down], out_hbm.at[down], sem.at[i])
        copy.start()
        copies.append(copy)
    for copy in copies:
        copy.wait()


def solution(mesh):
    n_row, n_col, n_fib = (mesh.shape[name] for name in ("row", "col", "fiber"))
    group = n_row // n_col

    def local(values, tile_mask, keep_mask):
        rows, unit = values.shape
        dma = pltpu.SemaphoreType.DMA
        squared, inverse = pl.pallas_call(
            functools.partial(kernel, n_row, n_col, n_fib),
            out_shape=(
                pltpu.VMEM((rows, unit), jnp.float32),
                pltpu.VMEM((8, unit), jnp.float32),
            ),
            in_specs=[
                pl.BlockSpec(memory_space=pltpu.HBM),
                pl.BlockSpec(memory_space=pltpu.HBM),
            ],
            out_specs=(
                pl.BlockSpec(memory_space=pltpu.VMEM),
                pl.BlockSpec(memory_space=pltpu.VMEM),
            ),
            scratch_shapes=[
                pltpu.SMEM(tile_mask.shape[::-1], jnp.int32),
                pltpu.VMEM((rows, unit), jnp.float32),
                pltpu.VMEM((n_fib, rows, unit), jnp.bfloat16),
                pltpu.VMEM((group * rows, n_col * unit), jnp.bfloat16),
                pltpu.VMEM((n_col, rows, unit), jnp.bfloat16),
                pltpu.VMEM((n_col, rows, unit), jnp.bfloat16),
                pltpu.VMEM((n_row, 8, unit), jnp.float32),
                dma((2,)),
                dma((n_fib, CHUNKS)),
                dma((n_fib, CHUNKS)),
                dma((n_fib, CHUNKS)),
                dma((n_row // group,)),
                dma((n_col,)),
                dma((n_col, group)),
                dma((n_col, group)),
                dma((n_col, CHUNKS)),
                dma((n_col, CHUNKS)),
                dma((n_row,)),
                dma((n_row,)),
            ],
            compiler_params=pltpu.CompilerParams(
                collective_id=0, has_side_effects=True, vmem_limit_bytes=VMEM_LIMIT
            ),
            name="expand",
        )(tile_mask.T, values)
        return pl.pallas_call(
            prune,
            out_shape=jax.ShapeDtypeStruct((rows, unit), jnp.float32),
            in_specs=[
                pl.BlockSpec(memory_space=pltpu.SMEM),
                pl.BlockSpec(memory_space=pltpu.VMEM),
                pl.BlockSpec(memory_space=pltpu.VMEM),
            ],
            out_specs=pl.BlockSpec(memory_space=pl.ANY),
            scratch_shapes=[
                pltpu.VMEM((rows, unit), jnp.float32),
                dma((keep_mask.shape[0],)),
            ],
            compiler_params=pltpu.CompilerParams(vmem_limit_bytes=8 * 1024 * 1024),
            name="prune",
        )(keep_mask.T, squared, inverse)

    spec = P("row", ("col", "fiber"))
    return jax.shard_map(
        local, mesh=mesh, in_specs=(spec, spec, spec), out_specs=spec, check_vma=False
    )
```

```python
import functools

import jax
import jax.numpy as jnp
from jax import lax
from jax.experimental import pallas as pl
from jax.experimental.pallas import tpu as pltpu
from jax.sharding import PartitionSpec as P

MESH = pl.DeviceIdType.MESH
CHUNKS = 6
EARLY = 3
BLOCKS = 3
LAG = 2
VMEM_LIMIT = 62 * 1024 * 1024


def kernel(
    n_row, n_col, n_fib, tile_hbm, values_hbm, own, inverse_ref,
    tile_ref, values_ref, left, right, ahead, part_out, part_in, sums, load_sem,
    send_up, send_down, recv_left, send_right, recv_right, send_pair, recv_pair,
    send_part, recv_part, send_sum, recv_sum,
):
    r, c, f = lax.axis_index("row"), lax.axis_index("col"), lax.axis_index("fiber")
    rows, unit = values_ref.shape
    tile = unit // tile_ref.shape[0]
    step = rows // CHUNKS
    group = n_row // n_col
    owner, seat = r // group, lax.rem(r, group)

    load = pltpu.make_async_copy(values_hbm, values_ref, load_sem.at[0])
    load.start()
    load_tile = pltpu.make_async_copy(tile_hbm, tile_ref, load_sem.at[1])
    load_tile.start()

    barrier = pltpu.get_barrier_semaphore()
    for dr in range(n_row):
        for dc in range(n_col):
            if dr or dc:
                pl.semaphore_signal(
                    barrier, inc=1, device_id_type=MESH,
                    device_id=(lax.rem(r + dr, n_row), lax.rem(c + dc, n_col), f),
                )

    has_down, has_up = f > 0, f < n_fib - 1

    @pl.when(has_down)
    def _():
        pl.semaphore_signal(barrier, inc=1, device_id=(r, c, f - 1), device_id_type=MESH)

    @pl.when(has_up)
    def _():
        pl.semaphore_signal(barrier, inc=1, device_id=(r, c, f + 1), device_id_type=MESH)

    load_tile.wait()
    load.wait()

    for i in range(rows // tile):
        for j in range(unit // tile):
            at = (pl.ds(i * tile, tile), pl.ds(j * tile, tile))
            masked = values_ref[at] * tile_ref[j, i].astype(jnp.float32)
            left[f, i * tile:(i + 1) * tile, j * tile:(j + 1) * tile] = masked.astype(jnp.bfloat16)

    neighbours = has_down.astype(jnp.int32) + has_up.astype(jnp.int32)
    pl.semaphore_wait(barrier, n_row * n_col - 1 + neighbours)

    def along(source, i, up):
        part = left.at[source, pl.ds(pl.multiple_of(i * step, step), step)]
        return pltpu.make_async_remote_copy(
            src_ref=part, dst_ref=part,
            send_sem=(send_up if up else send_down).at[source, i],
            recv_sem=recv_left.at[source, i],
            device_id=(r, c, f + 1 if up else f - 1), device_id_type=MESH,
        )

    def right_at(col, place):
        return right.at[
            pl.ds(pl.multiple_of(place * rows, rows), rows),
            pl.ds(pl.multiple_of(col * unit, unit), unit),
        ]

    def to_right(t):
        return pltpu.make_async_remote_copy(
            src_ref=left.at[f], dst_ref=right_at(c, seat),
            send_sem=send_right.at[t], recv_sem=recv_right.at[c],
            device_id=(t * group + seat, owner, f), device_id_type=MESH,
        )

    def came_right(col):
        return pltpu.make_async_remote_copy(
            src_ref=left.at[f], dst_ref=right_at(col, seat),
            send_sem=send_right.at[0], recv_sem=recv_right.at[col],
            device_id=(r, c, f), device_id_type=MESH,
        )

    def to_pair(col, other):
        return pltpu.make_async_remote_copy(
            src_ref=right_at(col, seat), dst_ref=right_at(col, seat),
            send_sem=send_pair.at[col, other], recv_sem=recv_pair.at[col, seat],
            device_id=(owner * group + other, c, f), device_id_type=MESH,
        )

    def came_pair(col, other):
        return pltpu.make_async_remote_copy(
            src_ref=right_at(col, other), dst_ref=right_at(col, other),
            send_sem=send_pair.at[col, other], recv_sem=recv_pair.at[col, other],
            device_id=(r, c, f), device_id_type=MESH,
        )

    def to_col(col, i):
        part = pl.ds(pl.multiple_of(i * step, step), step)
        return pltpu.make_async_remote_copy(
            src_ref=part_out.at[col, part], dst_ref=part_in.at[c, part],
            send_sem=send_part.at[col, i], recv_sem=recv_part.at[c, i],
            device_id=(r, col, f), device_id_type=MESH,
        )

    def came_col(col, i):
        part = pl.ds(pl.multiple_of(i * step, step), step)
        return pltpu.make_async_remote_copy(
            src_ref=part_out.at[col, part], dst_ref=part_in.at[col, part],
            send_sem=send_part.at[col, i], recv_sem=recv_part.at[col, i],
            device_id=(r, col, f), device_id_type=MESH,
        )

    @pl.loop(0, CHUNKS)
    def _(i):
        @pl.when(has_down)
        def _():
            along(f, i, False).start()

        @pl.when(has_up)
        def _():
            along(f, i, True).start()

    mine = owner == c
    for t in range(n_row // group):
        @pl.when(jnp.logical_not(mine & (owner == t)))
        def _():
            to_right(t).start()

    @pl.when(mine)
    def _():
        spot = right_at(c, seat)
        spot[...] = left[f]

    def relay(d, i):
        @pl.when(f - d >= 0)
        def _():
            along(f - d, i, True).wait_recv()

            @pl.when(has_up)
            def _():
                along(f - d, i, True).start()

        @pl.when(f + d < n_fib)
        def _():
            along(f + d, i, False).wait_recv()

            @pl.when(has_down)
            def _():
                along(f + d, i, False).start()

    def gather_right():
        for col in range(n_col):
            @pl.when(jnp.logical_not(mine & (c == col)))
            def _():
                came_right(col).wait_recv()

            for other in range(group):
                @pl.when(seat != other)
                def _():
                    to_pair(col, other).start()

    up_late, down_late = f + 1 == n_fib - 1, f - 1 == 0

    @pl.loop(0, CHUNKS)
    def _(i):
        @pl.when(has_down)
        def _():
            along(f - 1, i, True).wait_recv()

            @pl.when(has_up & (jnp.logical_not(up_late) | (i < EARLY)))
            def _():
                along(f - 1, i, True).start()

        @pl.when(has_up)
        def _():
            along(f + 1, i, False).wait_recv()

            @pl.when(has_down & (jnp.logical_not(down_late) | (i < EARLY)))
            def _():
                along(f + 1, i, False).start()

    gather_right()

    for col in range(n_col):
        for other in range(group):
            @pl.when(seat != other)
            def _():
                came_pair(col, other).wait_recv()

    first = jnp.where(has_down, f - 1, 0)
    ready = min(n_fib, 2)

    def product(part, shift, k):
        col = lax.rem(c + shift, n_col)
        return jnp.dot(
            left[k, part, :],
            right[
                pl.ds(pl.multiple_of(k * unit, unit), unit),
                pl.ds(pl.multiple_of(col * unit, unit), unit),
            ],
            preferred_element_type=jnp.float32,
        )

    def total_at(shift):
        return own if shift == 0 else ahead.at[shift - 1]

    @pl.loop(0, BLOCKS)
    def _(i):
        part = pl.ds(pl.multiple_of(i * (rows // BLOCKS), rows // BLOCKS), rows // BLOCKS)
        for shift in range(n_col):
            total = jnp.zeros((rows // BLOCKS, unit), jnp.float32)
            for k in range(ready):
                total += product(part, shift, lax.rem(first + k, n_fib))
            total_at(shift)[part, :] = total

    sums[r] = jnp.zeros((8, unit), jnp.float32)

    def combine(i):
        part = pl.ds(pl.multiple_of(i * step, step), step)
        expanded = own[part, :]
        for shift in range(1, n_col):
            col = lax.rem(c + shift, n_col)
            came_col(col, i).wait_recv()
            expanded += part_in[col, part, :].astype(jnp.float32)
        squared = expanded * expanded
        own[part, :] = squared
        sums[r] += jnp.sum(squared.reshape(step // 8, 8, unit), axis=0)

    @pl.loop(0, CHUNKS)
    def _(i):
        @pl.when(has_up & has_down & (i < CHUNKS - EARLY))
        def _():
            @pl.when(up_late)
            def _():
                along(f - 1, i + EARLY, True).start()

            @pl.when(down_late)
            def _():
                along(f + 1, i + EARLY, False).start()

        for d in range(2, n_fib):
            relay(d, i)
        part = pl.ds(pl.multiple_of(i * step, step), step)
        for shift in range(1, n_col):
            col = lax.rem(c + shift, n_col)
            total = ahead[shift - 1, part, :]
            for k in range(ready, n_fib):
                total += product(part, shift, lax.rem(first + k, n_fib))
            part_out[col, part, :] = total.astype(jnp.bfloat16)
            to_col(col, i).start()
        total = own[part, :]
        for k in range(ready, n_fib):
            total += product(part, 0, lax.rem(first + k, n_fib))
        own[part, :] = total

        @pl.when(i >= LAG)
        def _():
            combine(i - LAG)

    @pl.loop(CHUNKS - LAG, CHUNKS)
    def _(i):
        combine(i)

    def to_row(shift):
        return pltpu.make_async_remote_copy(
            src_ref=sums.at[r], dst_ref=sums.at[r],
            send_sem=send_sum.at[shift], recv_sem=recv_sum.at[r],
            device_id=(lax.rem(r + shift, n_row), c, f), device_id_type=MESH,
        )

    def came_row(other):
        return pltpu.make_async_remote_copy(
            src_ref=sums.at[r], dst_ref=sums.at[other],
            send_sem=send_sum.at[0], recv_sem=recv_sum.at[other],
            device_id=(other, c, f), device_id_type=MESH,
        )

    for shift in range(1, n_row):
        to_row(shift).start()
    for shift in range(1, n_row):
        came_row(lax.rem(r + shift, n_row)).wait_recv()
    total = sums[0]
    for other in range(1, n_row):
        total += sums[other]
    scale = jnp.sum(total, axis=0, keepdims=True) / (rows * n_row) + 1e-6
    inverse_ref[...] = jnp.broadcast_to(1.0 / scale, inverse_ref.shape)

    @pl.loop(0, CHUNKS)
    def _(i):
        for source in range(n_fib):
            @pl.when(has_up & (source <= f))
            def _():
                along(source, i, True).wait_send()

            @pl.when(has_down & (source >= f))
            def _():
                along(source, i, False).wait_send()

        for shift in range(1, n_col):
            to_col(lax.rem(c + shift, n_col), i).wait_send()

    for t in range(n_row // group):
        @pl.when(jnp.logical_not(mine & (owner == t)))
        def _():
            to_right(t).wait_send()

    for col in range(n_col):
        for other in range(group):
            @pl.when(seat != other)
            def _():
                to_pair(col, other).wait_send()

    for shift in range(1, n_row):
        to_row(shift).wait_send()


def prune(keep_ref, squared_ref, inverse_ref, out_hbm, out_vmem, sem):
    tile = out_vmem.shape[1] // keep_ref.shape[0]
    copies = []
    for i in range(keep_ref.shape[1]):
        down = slice(i * tile, (i + 1) * tile)
        for j in range(keep_ref.shape[0]):
            across = slice(j * tile, (j + 1) * tile)
            factor = inverse_ref[0:1, across] * keep_ref[j, i].astype(jnp.float32)
            out_vmem[down, across] = squared_ref[down, across] * factor
        copy = pltpu.make_async_copy(out_vmem.at[down], out_hbm.at[down], sem.at[i])
        copy.start()
        copies.append(copy)
    for copy in copies:
        copy.wait()


def solution(mesh):
    n_row, n_col, n_fib = (mesh.shape[name] for name in ("row", "col", "fiber"))
    group = n_row // n_col

    def local(values, tile_mask, keep_mask):
        rows, unit = values.shape
        dma = pltpu.SemaphoreType.DMA
        squared, inverse = pl.pallas_call(
            functools.partial(kernel, n_row, n_col, n_fib),
            out_shape=(
                pltpu.VMEM((rows, unit), jnp.float32),
                pltpu.VMEM((8, unit), jnp.float32),
            ),
            in_specs=[
                pl.BlockSpec(memory_space=pltpu.HBM),
                pl.BlockSpec(memory_space=pltpu.HBM),
            ],
            out_specs=(
                pl.BlockSpec(memory_space=pltpu.VMEM),
                pl.BlockSpec(memory_space=pltpu.VMEM),
            ),
            scratch_shapes=[
                pltpu.SMEM(tile_mask.shape[::-1], jnp.int32),
                pltpu.VMEM((rows, unit), jnp.float32),
                pltpu.VMEM((n_fib, rows, unit), jnp.bfloat16),
                pltpu.VMEM((group * rows, n_col * unit), jnp.bfloat16),
                pltpu.VMEM((n_col - 1, rows, unit), jnp.float32),
                pltpu.VMEM((n_col, rows, unit), jnp.bfloat16),
                pltpu.VMEM((n_col, rows, unit), jnp.bfloat16),
                pltpu.VMEM((n_row, 8, unit), jnp.float32),
                dma((2,)),
                dma((n_fib, CHUNKS)),
                dma((n_fib, CHUNKS)),
                dma((n_fib, CHUNKS)),
                dma((n_row // group,)),
                dma((n_col,)),
                dma((n_col, group)),
                dma((n_col, group)),
                dma((n_col, CHUNKS)),
                dma((n_col, CHUNKS)),
                dma((n_row,)),
                dma((n_row,)),
            ],
            compiler_params=pltpu.CompilerParams(
                collective_id=0, has_side_effects=True, vmem_limit_bytes=VMEM_LIMIT
            ),
            name="expand",
        )(tile_mask.T, values)
        return pl.pallas_call(
            prune,
            out_shape=jax.ShapeDtypeStruct((rows, unit), jnp.float32),
            in_specs=[
                pl.BlockSpec(memory_space=pltpu.SMEM),
                pl.BlockSpec(memory_space=pltpu.VMEM),
                pl.BlockSpec(memory_space=pltpu.VMEM),
            ],
            out_specs=pl.BlockSpec(memory_space=pl.ANY),
            scratch_shapes=[
                pltpu.VMEM((rows, unit), jnp.float32),
                dma((keep_mask.shape[0],)),
            ],
            compiler_params=pltpu.CompilerParams(vmem_limit_bytes=8 * 1024 * 1024),
            name="prune",
        )(keep_mask.T, squared, inverse)

    spec = P("row", ("col", "fiber"))
    return jax.shard_map(
        local, mesh=mesh, in_specs=(spec, spec, spec), out_specs=spec, check_vma=False
    )
```

```python
import functools

import jax
import jax.numpy as jnp
from jax import lax
from jax.experimental import pallas as pl
from jax.experimental.pallas import tpu as pltpu
from jax.sharding import PartitionSpec as P

MESH = pl.DeviceIdType.MESH
CHUNKS = 6
EARLY = 3
BLOCKS = 3
LAG = 2
VMEM_LIMIT = 62 * 1024 * 1024


def kernel(
    n_row, n_col, n_fib, tile_hbm, values_hbm, own, inverse_ref,
    tile_ref, values_ref, left, right, ahead, part_out, part_in, sums, load_sem,
    send_up, send_down, recv_left, send_right, recv_right, send_pair, recv_pair,
    send_part, recv_part, send_sum, recv_sum,
):
    r, c, f = lax.axis_index("row"), lax.axis_index("col"), lax.axis_index("fiber")
    rows, unit = values_ref.shape
    tile = unit // tile_ref.shape[0]
    step = rows // CHUNKS
    group = n_row // n_col
    owner, seat = r // group, lax.rem(r, group)

    load = pltpu.make_async_copy(values_hbm, values_ref, load_sem.at[0])
    load.start()
    load_tile = pltpu.make_async_copy(tile_hbm, tile_ref, load_sem.at[1])
    load_tile.start()

    barrier = pltpu.get_barrier_semaphore()
    for dr in range(n_row):
        for dc in range(n_col):
            if dr or dc:
                pl.semaphore_signal(
                    barrier, inc=1, device_id_type=MESH,
                    device_id=(lax.rem(r + dr, n_row), lax.rem(c + dc, n_col), f),
                )

    has_down, has_up = f > 0, f < n_fib - 1

    @pl.when(has_down)
    def _():
        pl.semaphore_signal(barrier, inc=1, device_id=(r, c, f - 1), device_id_type=MESH)

    @pl.when(has_up)
    def _():
        pl.semaphore_signal(barrier, inc=1, device_id=(r, c, f + 1), device_id_type=MESH)

    load_tile.wait()
    load.wait()

    for i in range(rows // tile):
        for j in range(unit // tile):
            at = (pl.ds(i * tile, tile), pl.ds(j * tile, tile))
            masked = values_ref[at] * tile_ref[j, i].astype(jnp.float32)
            left[f, i * tile:(i + 1) * tile, j * tile:(j + 1) * tile] = masked.astype(jnp.bfloat16)

    neighbours = has_down.astype(jnp.int32) + has_up.astype(jnp.int32)
    pl.semaphore_wait(barrier, n_row * n_col - 1 + neighbours)

    def along(source, i, up):
        part = left.at[source, pl.ds(pl.multiple_of(i * step, step), step)]
        return pltpu.make_async_remote_copy(
            src_ref=part, dst_ref=part,
            send_sem=(send_up if up else send_down).at[source, i],
            recv_sem=recv_left.at[source, i],
            device_id=(r, c, f + 1 if up else f - 1), device_id_type=MESH,
        )

    def right_at(col, place):
        return right.at[
            pl.ds(pl.multiple_of(place * rows, rows), rows),
            pl.ds(pl.multiple_of(col * unit, unit), unit),
        ]

    def to_right(t):
        return pltpu.make_async_remote_copy(
            src_ref=left.at[f], dst_ref=right_at(c, seat),
            send_sem=send_right.at[t], recv_sem=recv_right.at[c],
            device_id=(t * group + seat, owner, f), device_id_type=MESH,
        )

    def came_right(col):
        return pltpu.make_async_remote_copy(
            src_ref=left.at[f], dst_ref=right_at(col, seat),
            send_sem=send_right.at[0], recv_sem=recv_right.at[col],
            device_id=(r, c, f), device_id_type=MESH,
        )

    def to_pair(col, other):
        return pltpu.make_async_remote_copy(
            src_ref=right_at(col, seat), dst_ref=right_at(col, seat),
            send_sem=send_pair.at[col, other], recv_sem=recv_pair.at[col, seat],
            device_id=(owner * group + other, c, f), device_id_type=MESH,
        )

    def came_pair(col, other):
        return pltpu.make_async_remote_copy(
            src_ref=right_at(col, other), dst_ref=right_at(col, other),
            send_sem=send_pair.at[col, other], recv_sem=recv_pair.at[col, other],
            device_id=(r, c, f), device_id_type=MESH,
        )

    def to_col(col, i):
        part = pl.ds(pl.multiple_of(i * step, step), step)
        return pltpu.make_async_remote_copy(
            src_ref=part_out.at[col, part], dst_ref=part_in.at[c, part],
            send_sem=send_part.at[col, i], recv_sem=recv_part.at[c, i],
            device_id=(r, col, f), device_id_type=MESH,
        )

    def came_col(col, i):
        part = pl.ds(pl.multiple_of(i * step, step), step)
        return pltpu.make_async_remote_copy(
            src_ref=part_out.at[col, part], dst_ref=part_in.at[col, part],
            send_sem=send_part.at[col, i], recv_sem=recv_part.at[col, i],
            device_id=(r, col, f), device_id_type=MESH,
        )

    @pl.loop(0, CHUNKS)
    def _(i):
        @pl.when(has_down)
        def _():
            along(f, i, False).start()

        @pl.when(has_up)
        def _():
            along(f, i, True).start()

    mine = owner == c
    for t in range(n_row // group):
        @pl.when(jnp.logical_not(mine & (owner == t)))
        def _():
            to_right(t).start()

    @pl.when(mine)
    def _():
        spot = right_at(c, seat)
        spot[...] = left[f]

    def relay(d, i):
        @pl.when(f - d >= 0)
        def _():
            along(f - d, i, True).wait_recv()

            @pl.when(has_up)
            def _():
                along(f - d, i, True).start()

        @pl.when(f + d < n_fib)
        def _():
            along(f + d, i, False).wait_recv()

            @pl.when(has_down)
            def _():
                along(f + d, i, False).start()

    def gather_right():
        for col in range(n_col):
            @pl.when(jnp.logical_not(mine & (c == col)))
            def _():
                came_right(col).wait_recv()

            for other in range(group):
                @pl.when(seat != other)
                def _():
                    to_pair(col, other).start()

    up_late, down_late = f + 1 == n_fib - 1, f - 1 == 0

    @pl.loop(0, CHUNKS)
    def _(i):
        @pl.when(has_down)
        def _():
            along(f - 1, i, True).wait_recv()

            @pl.when(has_up & (jnp.logical_not(up_late) | (i < EARLY)))
            def _():
                along(f - 1, i, True).start()

        @pl.when(has_up)
        def _():
            along(f + 1, i, False).wait_recv()

            @pl.when(has_down & (jnp.logical_not(down_late) | (i < EARLY)))
            def _():
                along(f + 1, i, False).start()

    gather_right()

    for col in range(n_col):
        for other in range(group):
            @pl.when(seat != other)
            def _():
                came_pair(col, other).wait_recv()

    first = jnp.where(has_down, f - 1, 0)
    ready = min(n_fib, 2)

    def product(part, shift, k):
        col = lax.rem(c + shift, n_col)
        return jnp.dot(
            left[k, part, :],
            right[
                pl.ds(pl.multiple_of(k * unit, unit), unit),
                pl.ds(pl.multiple_of(col * unit, unit), unit),
            ],
            preferred_element_type=jnp.float32,
        )

    def total_at(shift):
        return own if shift == 0 else ahead.at[shift - 1]

    @pl.loop(0, BLOCKS)
    def _(i):
        part = pl.ds(pl.multiple_of(i * (rows // BLOCKS), rows // BLOCKS), rows // BLOCKS)
        for shift in range(n_col):
            total = jnp.zeros((rows // BLOCKS, unit), jnp.float32)
            for k in range(ready):
                total += product(part, shift, lax.rem(first + k, n_fib))
            total_at(shift)[part, :] = total

    sums[r] = jnp.zeros((8, unit), jnp.float32)

    def combine(i):
        part = pl.ds(pl.multiple_of(i * step, step), step)
        expanded = own[part, :]
        for shift in range(1, n_col):
            col = lax.rem(c + shift, n_col)
            came_col(col, i).wait_recv()
            expanded += part_in[col, part, :].astype(jnp.float32)
        squared = expanded * expanded
        own[part, :] = squared
        sums[r] += jnp.sum(squared.reshape(step // 8, 8, unit), axis=0)

    @pl.loop(0, CHUNKS)
    def _(i):
        for d in range(2, n_fib):
            relay(d, i)

        @pl.when(has_up & has_down & (i < CHUNKS - EARLY))
        def _():
            @pl.when(up_late)
            def _():
                along(f - 1, i + EARLY, True).start()

            @pl.when(down_late)
            def _():
                along(f + 1, i + EARLY, False).start()

        part = pl.ds(pl.multiple_of(i * step, step), step)
        for shift in range(1, n_col):
            col = lax.rem(c + shift, n_col)
            total = ahead[shift - 1, part, :]
            for k in range(ready, n_fib):
                total += product(part, shift, lax.rem(first + k, n_fib))
            part_out[col, part, :] = total.astype(jnp.bfloat16)
            to_col(col, i).start()
        total = own[part, :]
        for k in range(ready, n_fib):
            total += product(part, 0, lax.rem(first + k, n_fib))
        own[part, :] = total

        @pl.when(i >= LAG)
        def _():
            combine(i - LAG)

    @pl.loop(CHUNKS - LAG, CHUNKS)
    def _(i):
        combine(i)

    def to_row(shift):
        return pltpu.make_async_remote_copy(
            src_ref=sums.at[r], dst_ref=sums.at[r],
            send_sem=send_sum.at[shift], recv_sem=recv_sum.at[r],
            device_id=(lax.rem(r + shift, n_row), c, f), device_id_type=MESH,
        )

    def came_row(other):
        return pltpu.make_async_remote_copy(
            src_ref=sums.at[r], dst_ref=sums.at[other],
            send_sem=send_sum.at[0], recv_sem=recv_sum.at[other],
            device_id=(other, c, f), device_id_type=MESH,
        )

    for shift in range(1, n_row):
        to_row(shift).start()
    for shift in range(1, n_row):
        came_row(lax.rem(r + shift, n_row)).wait_recv()
    total = sums[0]
    for other in range(1, n_row):
        total += sums[other]
    scale = jnp.sum(total, axis=0, keepdims=True) / (rows * n_row) + 1e-6
    inverse_ref[...] = jnp.broadcast_to(1.0 / scale, inverse_ref.shape)

    @pl.loop(0, CHUNKS)
    def _(i):
        for source in range(n_fib):
            @pl.when(has_up & (source <= f))
            def _():
                along(source, i, True).wait_send()

            @pl.when(has_down & (source >= f))
            def _():
                along(source, i, False).wait_send()

        for shift in range(1, n_col):
            to_col(lax.rem(c + shift, n_col), i).wait_send()

    for t in range(n_row // group):
        @pl.when(jnp.logical_not(mine & (owner == t)))
        def _():
            to_right(t).wait_send()

    for col in range(n_col):
        for other in range(group):
            @pl.when(seat != other)
            def _():
                to_pair(col, other).wait_send()

    for shift in range(1, n_row):
        to_row(shift).wait_send()


def prune(keep_ref, squared_ref, inverse_ref, out_hbm, out_vmem, sem):
    tile = out_vmem.shape[1] // keep_ref.shape[0]
    copies = []
    for i in range(keep_ref.shape[1]):
        down = slice(i * tile, (i + 1) * tile)
        for j in range(keep_ref.shape[0]):
            across = slice(j * tile, (j + 1) * tile)
            factor = inverse_ref[0:1, across] * keep_ref[j, i].astype(jnp.float32)
            out_vmem[down, across] = squared_ref[down, across] * factor
        copy = pltpu.make_async_copy(out_vmem.at[down], out_hbm.at[down], sem.at[i])
        copy.start()
        copies.append(copy)
    for copy in copies:
        copy.wait()


def solution(mesh):
    n_row, n_col, n_fib = (mesh.shape[name] for name in ("row", "col", "fiber"))
    group = n_row // n_col

    def local(values, tile_mask, keep_mask):
        rows, unit = values.shape
        dma = pltpu.SemaphoreType.DMA
        squared, inverse = pl.pallas_call(
            functools.partial(kernel, n_row, n_col, n_fib),
            out_shape=(
                pltpu.VMEM((rows, unit), jnp.float32),
                pltpu.VMEM((8, unit), jnp.float32),
            ),
            in_specs=[
                pl.BlockSpec(memory_space=pltpu.HBM),
                pl.BlockSpec(memory_space=pltpu.HBM),
            ],
            out_specs=(
                pl.BlockSpec(memory_space=pltpu.VMEM),
                pl.BlockSpec(memory_space=pltpu.VMEM),
            ),
            scratch_shapes=[
                pltpu.SMEM(tile_mask.shape[::-1], jnp.int32),
                pltpu.VMEM((rows, unit), jnp.float32),
                pltpu.VMEM((n_fib, rows, unit), jnp.bfloat16),
                pltpu.VMEM((group * rows, n_col * unit), jnp.bfloat16),
                pltpu.VMEM((n_col - 1, rows, unit), jnp.float32),
                pltpu.VMEM((n_col, rows, unit), jnp.bfloat16),
                pltpu.VMEM((n_col, rows, unit), jnp.bfloat16),
                pltpu.VMEM((n_row, 8, unit), jnp.float32),
                dma((2,)),
                dma((n_fib, CHUNKS)),
                dma((n_fib, CHUNKS)),
                dma((n_fib, CHUNKS)),
                dma((n_row // group,)),
                dma((n_col,)),
                dma((n_col, group)),
                dma((n_col, group)),
                dma((n_col, CHUNKS)),
                dma((n_col, CHUNKS)),
                dma((n_row,)),
                dma((n_row,)),
            ],
            compiler_params=pltpu.CompilerParams(
                collective_id=0, has_side_effects=True, vmem_limit_bytes=VMEM_LIMIT
            ),
            name="expand",
        )(tile_mask.T, values)
        return pl.pallas_call(
            prune,
            out_shape=jax.ShapeDtypeStruct((rows, unit), jnp.float32),
            in_specs=[
                pl.BlockSpec(memory_space=pltpu.SMEM),
                pl.BlockSpec(memory_space=pltpu.VMEM),
                pl.BlockSpec(memory_space=pltpu.VMEM),
            ],
            out_specs=pl.BlockSpec(memory_space=pl.ANY),
            scratch_shapes=[
                pltpu.VMEM((rows, unit), jnp.float32),
                dma((keep_mask.shape[0],)),
            ],
            compiler_params=pltpu.CompilerParams(vmem_limit_bytes=8 * 1024 * 1024),
            name="prune",
        )(keep_mask.T, squared, inverse)

    spec = P("row", ("col", "fiber"))
    return jax.shard_map(
        local, mesh=mesh, in_specs=(spec, spec, spec), out_specs=spec, check_vma=False
    )
```
